32 devices in a mesh: cand: 16 (over z, x, core), tp: 2 (over y).
Axes of the slice: x: 2, y: 2, z: 4, core: 2. Of those that a mesh axis runs over, the one named last changes fastest.
Arguments:
- hidden_in: bfloat16 [128, 2, 8192], P('cand'), may hold values from -4 to 4
- queries: bfloat16 [128, 2, 32, 128], P('cand', None, 'tp'), may hold values from -128 to 128
- new_kv: bfloat16 [128, 2, 8, 2, 128], P('cand', None, 'tp'), may hold values from -5 to 5
- kv_cache: bfloat16 [128, 8, 2, 512, 128], P('cand', 'tp'), may hold values from -6 to 6
- lengths: int32 [128], P('cand'), may hold values from 128 to 512, as said below
- winner: int32 [8], replicated, may hold values from 0 to 15
- out_values: bfloat16 [4096, 8192], P('tp'), may hold values from -4 to 4
- out_scales: float32 [32, 64], P('tp'), may hold values from 0.008 to 0.032
Outputs:
- mixed: bfloat16 [128, 2, 8192], P('cand')
The draws below stay inside these ranges and needn't reach their ends.
Inputs may be any that keep to these rules, and one draw needn't show every extreme that they name: `lengths`: every draw has some row with exactly 512 live slots.
All inputs are finite; a program needn't handle non-finite values.
Results may differ from the reference program's by a relative error of at most 0.013.
Values may be sent and summed in bfloat16 or wider, within the bound.
A program may use at most 128 MiB of HBM per device.

```python
import math
import jax
import jax.numpy as jnp
from jax import lax

D = 8192
H = 32
KVH = 8
HD = 128
PROB = 8
CACHE = 512
BLOCK = 64
STEPS = 2
SB = 128
ROWS = 128
N_CAND = 16


def draw_kv_cache(key, part):
    shape = (ROWS, KVH, 2, CACHE, HD)
    filled = jnp.clip(jax.random.normal(jax.random.fold_in(key, 502), shape, jnp.float32), -5.0, 5.0)
    return filled.astype(jnp.bfloat16)


def draw_queries(key, part):
    shape = (ROWS, STEPS, H, HD)
    entries = jnp.clip(2.0 * jax.random.normal(jax.random.fold_in(key, 503), shape, jnp.float32), -12.0, 12.0)
    return entries.astype(jnp.bfloat16)


def draw_lengths(key, part):
    devices_count = ROWS // PROB
    tier = jax.random.randint(jax.random.fold_in(key, 506), (devices_count,), 1, 5)
    ceiling = jnp.maximum(2 * BLOCK, CACHE * tier // 4)
    per_row = jnp.repeat(ceiling, PROB)
    drawn = jax.random.randint(jax.random.fold_in(key, 507), (ROWS,), 2 * BLOCK, per_row + 1)
    longest = jax.random.randint(jax.random.fold_in(key, 508), (), 0, ROWS)
    return jnp.where(jnp.arange(ROWS) == longest, CACHE, drawn).astype(jnp.int32)


def place_ends(array, own_key, low, largest):
    longest = array.shape.index(max(array.shape))
    spots = []
    for shift in (0, 1):
        where = [jax.random.randint(jax.random.fold_in(own_key, axis), (), 0, length) for axis, length in enumerate(array.shape)]
        where[longest] = (where[longest] + shift) % array.shape[longest]
        spots.append(tuple(where))
    return array.at[spots[0]].set(low).at[spots[1]].set(largest)


def block_scale(stream_key, extent, shards, least, high):
    def one(dim, parts):
        steps = jax.random.uniform(jax.random.fold_in(jax.random.fold_in(stream_key, 6), dim), (parts,), jnp.float32, least / len(shards), high / len(shards))
        return jnp.repeat(jnp.exp(steps), extent[dim] // parts).reshape((-1,) + (1,) * (len(extent) - dim - 1))

    level = one(*shards[0])
    for cut in shards[1:]:
        level = level * one(*cut)
    return level


def scatter_about(rng, extent, width, reach, pieces=(), held_as=jnp.bfloat16):
    level = block_scale(rng, extent, pieces, -0.22, 0.18) if pieces else 1.0
    values = jax.random.normal(rng, extent, jnp.float32) * width * level
    return jnp.minimum(jnp.maximum(values, -reach), reach).astype(held_as)


def setup_inputs(seed: int = 0) -> dict:
    arg_keys = jax.random.split(jax.random.key(seed), 9)
    return {
        "hidden_in": scatter_about(arg_keys[0], (ROWS, STEPS, D), 0.5, 4.0, ((0, 16),)),
        "queries": draw_queries(jax.random.fold_in(arg_keys[8], 71), 0),
        "new_kv": scatter_about(arg_keys[2], (ROWS, STEPS, KVH, 2, HD), 1.0, 5.0, ((0, 16), (2, 2))),
        "kv_cache": draw_kv_cache(jax.random.fold_in(arg_keys[8], 71), 0),
        "lengths": draw_lengths(jax.random.fold_in(arg_keys[8], 71), 0),
        "winner": place_ends(jax.random.randint(arg_keys[5], (PROB,), 0, N_CAND), jax.random.fold_in(arg_keys[5], 1), 0, N_CAND - 1).astype(jnp.int32),
        "out_values": scatter_about(arg_keys[6], (H * HD, D), 1.0, 4.0, ((0, 2),)),
        "out_scales": jnp.clip(jnp.exp(math.log(0.032) - 1.3862944 * jax.random.uniform(arg_keys[7], (H * HD // SB, D // SB), jnp.float32) ** block_scale(arg_keys[7], (H * HD // SB, D // SB), ((0, 2),), -0.2, 0.2)), 0.008, 0.032),
    }


def reference(hidden_in, queries, new_kv, kv_cache, lengths, winner, out_values, out_scales):
    group = H // KVH
    factor = 1.0 / math.sqrt(HD)
    positions = jnp.arange(CACHE, dtype=jnp.int32)
    causal = jnp.arange(STEPS, dtype=jnp.int32)[None, :] <= jnp.arange(STEPS, dtype=jnp.int32)[:, None]

    def one_row(row):
        problem = row % PROB
        source = winner[problem] * PROB + problem
        src_len = lengths[source]
        own_len = lengths[row]
        block = lax.dynamic_slice_in_dim(kv_cache[source], (src_len - BLOCK).astype(jnp.int32), BLOCK, 2)
        cache = lax.dynamic_update_slice_in_dim(kv_cache[row], block, (own_len - BLOCK).astype(jnp.int32), 2)
        query = queries[row].astype(jnp.float32).reshape(STEPS, KVH, group, HD)
        fresh = jnp.transpose(new_kv[row], (1, 2, 0, 3))
        keys = jnp.concatenate([cache[:, 0], fresh[:, 0]], axis=1).astype(jnp.float32)
        values = jnp.concatenate([cache[:, 1], fresh[:, 1]], axis=1).astype(jnp.float32)
        scores = jnp.einsum('tkgd,kjd->tkgj', query, keys) * factor
        old_valid = jnp.broadcast_to(positions[None, :] < own_len, (STEPS, CACHE))
        valid = jnp.concatenate([old_valid, causal], axis=1)
        scores = jnp.where(valid[:, None, None, :], scores, -jnp.inf)
        peak = lax.optimization_barrier(jnp.max(scores, axis=-1, keepdims=True))
        expo = jnp.exp(scores - peak)
        weights = (expo / lax.optimization_barrier(jnp.sum(expo, axis=-1, keepdims=True))).astype(jnp.bfloat16)
        attended = jnp.einsum('tkgj,kjd->tkgd', weights.astype(jnp.float32), values)
        return attended.astype(jnp.bfloat16).reshape(STEPS, H * HD)
    attended = lax.map(one_row, jnp.arange(ROWS, dtype=jnp.int32))
    flat = attended.reshape(ROWS * STEPS, H * HD)

    def add_block(index, term):
        piece = lax.dynamic_slice_in_dim(flat, index * SB, SB, 1)
        weight_rows = lax.dynamic_slice_in_dim(out_values, index * SB, SB, 0)
        scale = jnp.repeat(lax.dynamic_index_in_dim(out_scales, index, 0, keepdims=False), SB)
        return term + jnp.dot(piece, weight_rows, preferred_element_type=jnp.float32) * scale[None, :]
    term = lax.fori_loop(0, H * HD // SB, add_block, jnp.zeros((ROWS * STEPS, D), jnp.float32))
    result = (hidden_in.reshape(ROWS * STEPS, D).astype(jnp.float32) + term).astype(jnp.bfloat16)
    return result.reshape(ROWS, STEPS, D)
```

```python
import functools
import math

import jax
import jax.numpy as jnp
from jax import lax
from jax.experimental import pallas as pl
from jax.experimental.pallas import tpu as pltpu
from jax.sharding import PartitionSpec as P

BLOCK = 64
PAD = 16
LOW = -1e30
MESH = pl.DeviceIdType.MESH


def kernel(
    cand_n, tp_n, tile, split,
    lengths, winner, scales, queries, fresh, hidden, cache_hbm, weights_hbm, out,
    cache, weights, first, got, own, near0, up0, far0, down0, mid, near1, up1, far1, down1,
    fork, top_s, sum_s, acc_s, att, lhs, parts,
    cache_sem, weight_sem, send_sem, recv_sem, part_send, part_recv,
):
    me = lax.axis_index("cand")
    tp_me = lax.axis_index("tp")
    problems, kv_here, _, slots, head_dim = cache.shape
    steps_heads = queries.shape[1]
    heads = weights.shape[0] // head_dim
    steps = steps_heads // heads
    group = heads // kv_here
    rows = problems * steps
    half = problems // 2
    hs = kv_here // split
    chunks = half * split
    core = lax.rem(me, 2)
    chip = lax.div(me, 2)
    outer_len = 4
    inner_len = cand_n // 2 // outer_len
    inner_at = lax.rem(chip, inner_len)
    outer_at = lax.div(chip, inner_len)
    sibling = me + 1 - 2 * core

    def ends(at, length, stride):
        low_side = at < length // 2
        step = jnp.where(low_side, stride, -stride)
        has_near = jnp.logical_and(at > 0, at < length - 1)
        crosses = jnp.logical_or(at == length // 2 - 1, at == length // 2)
        return has_near, crosses, me + step, me - step

    inner = ends(inner_at, inner_len, 2)
    outer = ends(outer_at, outer_len, 2 * inner_len)

    barrier = pltpu.get_barrier_semaphore()

    def greet(**where):
        pl.semaphore_signal(barrier, inc=1, device_id=where, device_id_type=MESH)

    greet(cand=sibling)
    count = 1 + (tp_n - 1)
    for has_near, _, far, near in (inner, outer):
        greet(cand=far)

        @pl.when(has_near)
        def _(near=near):
            greet(cand=near)

        count = count + 1 + has_near.astype(jnp.int32)
    for k in range(1, tp_n):
        greet(tp=lax.rem(tp_me + k, tp_n))

    pieces = weight_sem.shape[0]
    piece = weights.shape[0] // pieces

    def cache_copy(p):
        return pltpu.make_async_copy(cache_hbm.at[p], cache.at[p], cache_sem.at[p])

    def weight_copy(i):
        at = pl.ds(i * piece, piece)
        return pltpu.make_async_copy(weights_hbm.at[at], weights.at[at], weight_sem.at[i])

    for p in range(problems):
        cache_copy(p).start()
    for i in range(pieces):
        weight_copy(i).start()
    for p in range(problems):
        cache_copy(p).wait()
    pl.semaphore_wait(barrier, count)

    def remote(src, dst, kind, j, target):
        return pltpu.make_async_remote_copy(
            src_ref=src, dst_ref=dst, send_sem=send_sem.at[kind, j],
            recv_sem=recv_sem.at[kind, j], device_id={"cand": target}, device_id_type=MESH,
        )

    row_i = lax.broadcasted_iota(jnp.int32, (BLOCK, slots), 0)
    col_i = lax.broadcasted_iota(jnp.int32, (BLOCK, slots), 1)

    def extract(p, sub, put):
        shift = jnp.where(winner[p] == me, lengths[p] - BLOCK, 2 * slots)
        pick = (col_i == row_i + shift).astype(jnp.float32).astype(jnp.bfloat16)
        for h in range(hs):
            for kv in range(2):
                put(h, kv, jnp.dot(pick, cache[p, sub * hs + h, kv], preferred_element_type=jnp.float32).astype(jnp.bfloat16))

    def sibling_copy(j):
        return remote(first.at[j], got.at[j], 0, j, sibling)

    def give(j, carry):
        def put(h, kv, value):
            first[j, h, kv] = value

        extract((1 - core) * half + lax.div(j, split), lax.rem(j, split), put)
        sibling_copy(j).start()
        return carry

    lax.fori_loop(0, chunks, give, 0)

    def keep(j, carry):
        def put(h, kv, value):
            own[j, h, kv] = value

        extract(core * half + lax.div(j, split), lax.rem(j, split), put)
        return carry

    lax.fori_loop(0, chunks, keep, 0)

    def make_line(line, kind, base_ref, near_ref, up_ref, far_ref, down_ref):
        has_near, crosses, far_id, near_id = line

        def to_far_in(j):
            return remote(up_ref.at[j], near_ref.at[j], kind, j, far_id)

        def to_far_cross(j):
            return remote(up_ref.at[j], far_ref.at[j], kind + 1, j, far_id)

        def to_near(j):
            return remote(down_ref.at[j], far_ref.at[j], kind + 1, j, near_id)

        def climb(j):
            @pl.when(has_near)
            def _():
                to_far_in(j).wait_recv()
                up_ref[j] = base_ref[j] + near_ref[j]

            @pl.when(jnp.logical_not(has_near))
            def _():
                up_ref[j] = base_ref[j]

            @pl.when(crosses)
            def _():
                to_far_cross(j).start()

            @pl.when(jnp.logical_not(crosses))
            def _():
                to_far_in(j).start()

        def settle(j):
            to_far_cross(j).wait_recv()

            @pl.when(has_near)
            def _():
                down_ref[j] = base_ref[j] + far_ref[j]
                pltpu.make_async_remote_copy(
                    src_ref=down_ref.at[j], dst_ref=far_ref.at[j], send_sem=send_sem.at[kind + 2, j],
                    recv_sem=recv_sem.at[kind + 1, j], device_id={"cand": near_id}, device_id_type=MESH,
                ).start()

            return up_ref[j] + far_ref[j]

        def drain(j):
            @pl.when(crosses)
            def _():
                to_far_cross(j).wait_send()

            @pl.when(jnp.logical_not(crosses))
            def _():
                to_far_in(j).wait_send()

            @pl.when(has_near)
            def _():
                remote(down_ref.at[j], far_ref.at[j], kind + 2, j, near_id).wait_send()

        return climb, settle, drain

    climb0, settle0, drain0 = make_line(inner, 1, own, near0, up0, far0, down0)
    climb1, settle1, drain1 = make_line(outer, 4, mid, near1, up1, far1, down1)

    def loop(body):
        def step(j, carry):
            body(j)
            return carry

        lax.fori_loop(0, chunks, step, 0)

    def enter(j):
        sibling_copy(j).wait_recv()
        own[j] = own[j] + got[j]
        climb0(j)

    loop(enter)

    factor = 1.0 / math.sqrt(head_dim)

    def row_of(width):
        return lax.broadcasted_iota(jnp.int32, (steps_heads, width), 0)

    def col_of(width):
        return lax.broadcasted_iota(jnp.int32, (steps_heads, width), 1)

    def score(q, keys):
        return lax.dot_general(q, keys, (((1,), (1,)), ((), ())), preferred_element_type=jnp.float32) * factor

    def local_part(p):
        q = queries[p]
        s = score(q, cache[p, :, 0].reshape(kv_here * slots, head_dim))
        row, col = row_of(kv_here * slots), col_of(kv_here * slots)
        mine = lax.div(lax.rem(row, heads), group) == lax.div(col, slots)
        s = jnp.where(jnp.logical_and(mine, lax.rem(col, slots) < lengths[p] - BLOCK), s, LOW)
        n = score(q, fresh[p, 0])
        width = fresh.shape[2]
        row, col = row_of(width), col_of(width)
        mine = lax.div(lax.rem(row, heads), group) == lax.div(col, PAD)
        n = jnp.where(jnp.logical_and(mine, lax.rem(col, PAD) <= lax.div(row, heads)), n, LOW)
        top = jnp.maximum(jnp.max(s, 1, keepdims=True), jnp.max(n, 1, keepdims=True))
        s = jnp.exp(s - top)
        n = jnp.exp(n - top)
        top_s[p] = jnp.broadcast_to(top, (steps_heads, head_dim))
        sum_s[p] = jnp.broadcast_to(jnp.sum(s, 1, keepdims=True) + jnp.sum(n, 1, keepdims=True), (steps_heads, head_dim))
        acc_s[p] = jnp.dot(
            s.astype(jnp.bfloat16), cache[p, :, 1].reshape(kv_here * slots, head_dim),
            preferred_element_type=jnp.float32,
        ) + jnp.dot(n.astype(jnp.bfloat16), fresh[p, 1], preferred_element_type=jnp.float32)

    def local_parts(start, stop):
        def step(p, carry):
            local_part(p)
            return carry

        lax.fori_loop(start, stop, step, 0)

    local_parts(0, half)

    def turn(j):
        mid[j] = settle0(j)
        climb1(j)

    loop(turn)
    local_parts(half, problems)

    def fork_copy(j):
        at = core * chunks + j
        return remote(fork.at[at], fork.at[at], 7, j, sibling)

    def finish(j):
        fork[core * chunks + j] = settle1(j)
        fork_copy(j).start()

    loop(finish)

    def closing(j):
        remote(first.at[j], fork.at[(1 - core) * chunks + j], 7, j, sibling).wait_recv()

    loop(closing)

    def fork_part(p, carry):
        q = queries[p]
        both = fork[pl.ds(p * split, split)]
        keys = both[:, :, 0].reshape(kv_here * BLOCK, head_dim)
        values = both[:, :, 1].reshape(kv_here * BLOCK, head_dim)
        s = score(q, keys)
        row, col = row_of(kv_here * BLOCK), col_of(kv_here * BLOCK)
        mine = lax.div(lax.rem(row, heads), group) == lax.div(col, BLOCK)
        s = jnp.where(mine, s, LOW)
        before = top_s[p]
        top = jnp.maximum(before, jnp.max(s, 1, keepdims=True))
        s = jnp.exp(s - top[:, :1])
        scale = jnp.exp(before - top)
        total = sum_s[p] * scale + jnp.sum(s, 1, keepdims=True)
        acc = acc_s[p] * scale + jnp.dot(s.astype(jnp.bfloat16), values, preferred_element_type=jnp.float32)
        att[pl.ds(p * steps_heads, steps_heads), :] = acc / total
        return carry

    lax.fori_loop(0, problems, fork_part, 0)

    pairs = heads // 2
    empty = jnp.zeros((rows, head_dim), jnp.bfloat16)
    for i in range(pairs):
        a = att[pl.ds(2 * i, rows, stride=heads), :].astype(jnp.bfloat16)
        b = att[pl.ds(2 * i + 1, rows, stride=heads), :].astype(jnp.bfloat16)
        lhs[i] = jnp.concatenate(
            [jnp.concatenate([a, empty], 1), jnp.concatenate([empty, b], 1)], 0
        )

    for i in range(pieces):
        weight_copy(i).wait()

    tiles = parts.shape[1]
    per = tile // head_dim

    def part_copy(t, k):
        return pltpu.make_async_remote_copy(
            src_ref=parts.at[tp_me, t], dst_ref=parts.at[tp_me, t], send_sem=part_send.at[k - 1, t],
            recv_sem=part_recv.at[tp_me, t], device_id={"tp": lax.rem(tp_me + k, tp_n)},
            device_id_type=MESH,
        )

    def project(t, carry):
        at = pl.ds(pl.multiple_of(t * tile, tile), tile)
        total = [jnp.zeros((rows, head_dim), jnp.float32) for _ in range(per)]
        for i in range(pairs):
            product = jnp.dot(
                lhs[i], weights[pl.ds(2 * i * head_dim, 2 * head_dim), at], preferred_element_type=jnp.float32
            )
            for c in range(per):
                here = product[:, c * head_dim:(c + 1) * head_dim]
                total[c] = (
                    total[c] + here[:rows] * scales[2 * i, t * per + c]
                    + here[rows:] * scales[2 * i + 1, t * per + c]
                )
        parts[tp_me, t] = jnp.concatenate(total, 1).astype(jnp.bfloat16)
        for k in range(1, tp_n):
            part_copy(t, k).start()
        return carry

    lax.fori_loop(0, tiles, project, 0)

    def gather(t, carry):
        at = pl.ds(pl.multiple_of(t * tile, tile), tile)
        for k in range(1, tp_n):
            source = lax.rem(tp_me + k, tp_n)
            pltpu.make_async_remote_copy(
                src_ref=parts.at[tp_me, t], dst_ref=parts.at[source, t], send_sem=part_send.at[k - 1, t],
                recv_sem=part_recv.at[source, t], device_id={"tp": source}, device_id_type=MESH,
            ).wait_recv()
        total = parts[0, t].astype(jnp.float32)
        for k in range(1, tp_n):
            total = total + parts[k, t].astype(jnp.float32)
        out[:, at] = (hidden[:, at].astype(jnp.float32) + total).astype(jnp.bfloat16)
        return carry

    lax.fori_loop(0, tiles, gather, 0)

    def rest(j):
        sibling_copy(j).wait_send()
        drain0(j)
        drain1(j)
        fork_copy(j).wait_send()

    loop(rest)

    def rest_parts(t, carry):
        for k in range(1, tp_n):
            part_copy(t, k).wait_send()
        return carry

    lax.fori_loop(0, tiles, rest_parts, 0)


def local(cand_n, tp_n, hidden_in, queries, new_kv, kv_cache, lengths, winner, out_values, out_scales):
    problems, kv_here, _, slots, head_dim = kv_cache.shape
    steps, heads = queries.shape[1:3]
    depth, width = out_values.shape
    rows = problems * steps
    split = 2 if kv_here % 2 == 0 else 1
    chunks = problems // 2 * split
    tile = 512
    tiles = width // tile
    flat = queries.reshape(problems, steps * heads, head_dim)
    fresh = jnp.transpose(new_kv, (0, 3, 2, 1, 4))
    fresh = jnp.pad(fresh, ((0, 0), (0, 0), (0, 0), (0, PAD - steps), (0, 0)))
    fresh = fresh.reshape(problems, 2, kv_here * PAD, head_dim)
    smem = pl.BlockSpec(memory_space=pltpu.SMEM)
    vmem = pl.BlockSpec(memory_space=pltpu.VMEM)
    hbm = pl.BlockSpec(memory_space=pl.ANY)
    line = pltpu.VMEM((chunks, kv_here // split, 2, BLOCK, head_dim), jnp.bfloat16)
    stat = pltpu.VMEM((problems, steps * heads, head_dim), jnp.float32)
    dma = pltpu.SemaphoreType.DMA
    out = pl.pallas_call(
        functools.partial(kernel, cand_n, tp_n, tile, split),
        out_shape=jax.ShapeDtypeStruct((rows, width), jnp.bfloat16),
        in_specs=[smem, smem, smem, vmem, vmem, vmem, hbm, hbm],
        out_specs=vmem,
        scratch_shapes=[
            pltpu.VMEM(kv_cache.shape, jnp.bfloat16),
            pltpu.VMEM(out_values.shape, jnp.bfloat16),
            *[line] * 12,
            pltpu.VMEM((problems * split, kv_here // split, 2, BLOCK, head_dim), jnp.bfloat16),
            stat, stat, stat,
            pltpu.VMEM((problems * steps * heads, head_dim), jnp.float32),
            pltpu.VMEM((heads // 2, 2 * rows, 2 * head_dim), jnp.bfloat16),
            pltpu.VMEM((tp_n, tiles, rows, tile), jnp.bfloat16),
            dma((problems,)), dma((8,)), dma((8, chunks)), dma((8, chunks)),
            dma((max(tp_n - 1, 1), tiles)), dma((tp_n, tiles)),
        ],
        compiler_params=pltpu.CompilerParams(
            collective_id=0, has_side_effects=True, vmem_limit_bytes=67043328 - (2 << 20)
        ),
    )(lengths, winner, out_scales, flat, fresh, hidden_in.reshape(rows, width), kv_cache, out_values)
    return out.reshape(hidden_in.shape)


def solution(mesh):
    placed = (
        P("cand", None, None),
        P("cand", None, "tp", None),
        P("cand", None, "tp", None, None),
        P("cand", "tp", None, None, None),
        P("cand"),
        P(),
        P("tp", None),
        P("tp", None),
    )
    return jax.shard_map(
        functools.partial(local, mesh.shape["cand"], mesh.shape["tp"]),
        mesh=mesh, in_specs=placed, out_specs=P("cand", None, None), check_vma=False,
    )
```

```python
import functools
import math

import jax
import jax.numpy as jnp
from jax import lax
from jax.experimental import pallas as pl
from jax.experimental.pallas import tpu as pltpu
from jax.sharding import PartitionSpec as P

BLOCK = 64
WINDOW = 128
LAG = 3
PAD = 16
LOW = -1e30
MESH = pl.DeviceIdType.MESH


def pick_kernel(lengths, winner, cache_hbm, blocks, held, sem):
    problems, kv_here, _, window, _ = held.shape
    slots = cache_hbm.shape[3]
    hs = blocks.shape[1]
    split = kv_here // hs
    me = lax.axis_index("cand")

    def begin_of(p):
        begin = lengths[p] - BLOCK
        base = jnp.clip(lax.div(begin, PAD) * PAD, 0, slots - window)
        return begin, pl.multiple_of(base, PAD)

    def fetch(p):
        base = begin_of(p)[1]
        return pltpu.make_async_copy(
            cache_hbm.at[p, :, :, pl.ds(base, window), :], held.at[p], sem.at[p]
        )

    for p in range(problems):
        fetch(p).start()
    row = lax.broadcasted_iota(jnp.int32, (BLOCK, window), 0)
    col = lax.broadcasted_iota(jnp.int32, (BLOCK, window), 1)
    for p in range(problems):
        fetch(p).wait()
        begin, base = begin_of(p)
        shift = jnp.where(winner[p] == me, begin - base, 4 * window)
        pick = (col == row + shift).astype(jnp.float32).astype(jnp.bfloat16)
        for h in range(kv_here):
            for kv in range(2):
                blocks[p * split + h // hs, h % hs, kv] = jnp.dot(
                    pick, held[p, h, kv], preferred_element_type=jnp.float32
                ).astype(jnp.bfloat16)


def kernel(
    cand_n, tp_n, tile, split,
    lengths, scales, blocks, queries, fresh, hidden, cache_hbm, weights_hbm, out,
    cache, weights, got, own, near0, up0, far0, down0, mid, near1, up1, far1, down1,
    fork, top_s, sum_s, acc_s, att, lhs, parts,
    cache_sem, weight_sem, send_sem, recv_sem, part_send, part_recv,
):
    me = lax.axis_index("cand")
    tp_me = lax.axis_index("tp")
    problems, kv_here, _, slots, head_dim = cache.shape
    steps_heads = queries.shape[1]
    heads = weights.shape[0] // head_dim
    steps = steps_heads // heads
    group = heads // kv_here
    rows = problems * steps
    half = problems // 2
    hs = kv_here // split
    chunks = half * split
    core = lax.rem(me, 2)
    chip = lax.div(me, 2)
    outer_len = 4
    inner_len = cand_n // 2 // outer_len
    inner_at = lax.rem(chip, inner_len)
    outer_at = lax.div(chip, inner_len)
    sibling = me + 1 - 2 * core

    def ends(at, length, stride):
        low_side = at < length // 2
        step = jnp.where(low_side, stride, -stride)
        has_near = jnp.logical_and(at > 0, at < length - 1)
        crosses = jnp.logical_or(at == length // 2 - 1, at == length // 2)
        return has_near, crosses, me + step, me - step

    inner = ends(inner_at, inner_len, 2)
    outer = ends(outer_at, outer_len, 2 * inner_len)

    barrier = pltpu.get_barrier_semaphore()

    def greet(**where):
        pl.semaphore_signal(barrier, inc=1, device_id=where, device_id_type=MESH)

    greet(cand=sibling)
    count = 1 + (tp_n - 1)
    for has_near, _, far, near in (inner, outer):
        greet(cand=far)

        @pl.when(has_near)
        def _(near=near):
            greet(cand=near)

        count = count + 1 + has_near.astype(jnp.int32)
    for k in range(1, tp_n):
        greet(tp=lax.rem(tp_me + k, tp_n))

    pieces = weight_sem.shape[0]
    piece = weights.shape[0] // pieces

    def cache_copy(p):
        return pltpu.make_async_copy(cache_hbm.at[p], cache.at[p], cache_sem.at[p])

    def weight_copy(i):
        at = pl.ds(i * piece, piece)
        return pltpu.make_async_copy(weights_hbm.at[at], weights.at[at], weight_sem.at[i])

    for p in range(problems):
        cache_copy(p).start()
    pl.semaphore_wait(barrier, count)

    def remote(src, dst, kind, j, target):
        return pltpu.make_async_remote_copy(
            src_ref=src, dst_ref=dst, send_sem=send_sem.at[kind, j],
            recv_sem=recv_sem.at[kind, j], device_id={"cand": target}, device_id_type=MESH,
        )

    def sibling_copy(j):
        return remote(blocks.at[(1 - core) * chunks + j], got.at[j], 0, j, sibling)

    def loop(body, length):
        def step(j, carry):
            body(j)
            return carry

        lax.fori_loop(0, length, step, 0)

    loop(lambda j: sibling_copy(j).start(), chunks)

    def make_line(line, kind, base_ref, near_ref, up_ref, far_ref, down_ref):
        has_near, crosses, far_id, near_id = line

        def to_far_in(j):
            return remote(up_ref.at[j], near_ref.at[j], kind, j, far_id)

        def to_far_cross(j):
            return remote(up_ref.at[j], far_ref.at[j], kind + 1, j, far_id)

        def to_near(j):
            return remote(down_ref.at[j], far_ref.at[j], kind + 1, j, near_id)

        def climb(j):
            @pl.when(has_near)
            def _():
                to_far_in(j).wait_recv()
                up_ref[j] = base_ref[j] + near_ref[j]

            @pl.when(jnp.logical_not(has_near))
            def _():
                up_ref[j] = base_ref[j]

            @pl.when(crosses)
            def _():
                to_far_cross(j).start()

            @pl.when(jnp.logical_not(crosses))
            def _():
                to_far_in(j).start()

        def settle(j):
            to_far_cross(j).wait_recv()

            @pl.when(has_near)
            def _():
                down_ref[j] = base_ref[j] + far_ref[j]
                pltpu.make_async_remote_copy(
                    src_ref=down_ref.at[j], dst_ref=far_ref.at[j], send_sem=send_sem.at[kind + 2, j],
                    recv_sem=recv_sem.at[kind + 1, j], device_id={"cand": near_id}, device_id_type=MESH,
                ).start()

            return up_ref[j] + far_ref[j]

        def drain(j):
            @pl.when(crosses)
            def _():
                to_far_cross(j).wait_send()

            @pl.when(jnp.logical_not(crosses))
            def _():
                to_far_in(j).wait_send()

            @pl.when(has_near)
            def _():
                remote(down_ref.at[j], far_ref.at[j], kind + 2, j, near_id).wait_send()

        return climb, settle, drain

    climb0, settle0, drain0 = make_line(inner, 1, own, near0, up0, far0, down0)
    climb1, settle1, drain1 = make_line(outer, 4, mid, near1, up1, far1, down1)

    def enter(j):
        sibling_copy(j).wait_recv()
        own[j] = blocks[core * chunks + j] + got[j]
        climb0(j)

    loop(enter, chunks)
    for i in range(pieces):
        weight_copy(i).start()

    factor = 1.0 / math.sqrt(head_dim)

    def row_of(width):
        return lax.broadcasted_iota(jnp.int32, (steps_heads, width), 0)

    def col_of(width):
        return lax.broadcasted_iota(jnp.int32, (steps_heads, width), 1)

    def score(q, keys):
        return lax.dot_general(q, keys, (((1,), (1,)), ((), ())), preferred_element_type=jnp.float32) * factor

    def local_part(p):
        cache_copy(p).wait()
        q = queries[p]
        s = score(q, cache[p, :, 0].reshape(kv_here * slots, head_dim))
        row, col = row_of(kv_here * slots), col_of(kv_here * slots)
        mine = lax.div(lax.rem(row, heads), group) == lax.div(col, slots)
        s = jnp.where(jnp.logical_and(mine, lax.rem(col, slots) < lengths[p] - BLOCK), s, LOW)
        n = score(q, fresh[p, 0])
        width = fresh.shape[2]
        row, col = row_of(width), col_of(width)
        mine = lax.div(lax.rem(row, heads), group) == lax.div(col, steps)
        n = jnp.where(jnp.logical_and(mine, lax.rem(col, steps) <= lax.div(row, heads)), n, LOW)
        top = jnp.maximum(jnp.max(s, 1, keepdims=True), jnp.max(n, 1, keepdims=True))
        s = jnp.exp(s - top)
        n = jnp.exp(n - top)
        top_s[p] = jnp.broadcast_to(top, (steps_heads, head_dim))
        sum_s[p] = jnp.broadcast_to(jnp.sum(s, 1, keepdims=True) + jnp.sum(n, 1, keepdims=True), (steps_heads, head_dim))
        acc_s[p] = jnp.dot(
            s.astype(jnp.bfloat16), cache[p, :, 1].reshape(kv_here * slots, head_dim),
            preferred_element_type=jnp.float32,
        ) + jnp.dot(n.astype(jnp.bfloat16), fresh[p, 1], preferred_element_type=jnp.float32)

    def turn(j):
        mid[j] = settle0(j)
        climb1(j)


    def fork_copy(j):
        at = core * chunks + j
        return remote(fork.at[at], fork.at[at], 7, j, sibling)

    def finish(j):
        fork[core * chunks + j] = settle1(j)
        fork_copy(j).start()

    each = pl.cdiv(problems, chunks)

    def advance(j):
        @pl.when(j < chunks)
        def _():
            turn(j)

        for i in range(each):
            @pl.when(j * each + i < problems)
            def _(i=i):
                local_part(j * each + i)

        @pl.when(j >= LAG)
        def _():
            finish(j - LAG)

    loop(advance, chunks + LAG)

    def closing(j):
        remote(got.at[j], fork.at[(1 - core) * chunks + j], 7, j, sibling).wait_recv()

    loop(closing, chunks)

    def fork_part(p, carry):
        q = queries[p]
        both = fork[pl.ds(p * split, split)]
        keys = both[:, :, 0].reshape(kv_here * BLOCK, head_dim)
        values = both[:, :, 1].reshape(kv_here * BLOCK, head_dim)
        s = score(q, keys)
        row, col = row_of(kv_here * BLOCK), col_of(kv_here * BLOCK)
        mine = lax.div(lax.rem(row, heads), group) == lax.div(col, BLOCK)
        s = jnp.where(mine, s, LOW)
        before = top_s[p]
        top = jnp.maximum(before, jnp.max(s, 1, keepdims=True))
        s = jnp.exp(s - top[:, :1])
        scale = jnp.exp(before - top)
        total = sum_s[p] * scale + jnp.sum(s, 1, keepdims=True)
        acc = acc_s[p] * scale + jnp.dot(s.astype(jnp.bfloat16), values, preferred_element_type=jnp.float32)
        att[pl.ds(p * steps_heads, steps_heads), :] = acc / total
        return carry

    lax.fori_loop(0, problems, fork_part, 0)

    pairs = heads // 2
    empty = jnp.zeros((rows, head_dim), jnp.bfloat16)
    for i in range(pairs):
        a = att[pl.ds(2 * i, rows, stride=heads), :].astype(jnp.bfloat16)
        b = att[pl.ds(2 * i + 1, rows, stride=heads), :].astype(jnp.bfloat16)
        lhs[i] = jnp.concatenate(
            [jnp.concatenate([a, empty], 1), jnp.concatenate([empty, b], 1)], 0
        )

    for i in range(pieces):
        weight_copy(i).wait()

    tiles = parts.shape[1]
    per = tile // head_dim

    def part_copy(t, k):
        return pltpu.make_async_remote_copy(
            src_ref=parts.at[tp_me, t], dst_ref=parts.at[tp_me, t], send_sem=part_send.at[k - 1, t],
            recv_sem=part_recv.at[tp_me, t], device_id={"tp": lax.rem(tp_me + k, tp_n)},
            device_id_type=MESH,
        )

    def project(t, carry):
        at = pl.ds(pl.multiple_of(t * tile, tile), tile)
        total = [jnp.zeros((rows, head_dim), jnp.float32) for _ in range(per)]
        for i in range(pairs):
            product = jnp.dot(
                lhs[i], weights[pl.ds(2 * i * head_dim, 2 * head_dim), at], preferred_element_type=jnp.float32
            )
            for c in range(per):
                here = product[:, c * head_dim:(c + 1) * head_dim]
                total[c] = (
                    total[c] + here[:rows] * scales[2 * i, t * per + c]
                    + here[rows:] * scales[2 * i + 1, t * per + c]
                )
        parts[tp_me, t] = jnp.concatenate(total, 1).astype(jnp.bfloat16)
        for k in range(1, tp_n):
            part_copy(t, k).start()
        return carry

    lax.fori_loop(0, tiles, project, 0)

    def gather(t, carry):
        at = pl.ds(pl.multiple_of(t * tile, tile), tile)
        for k in range(1, tp_n):
            source = lax.rem(tp_me + k, tp_n)
            pltpu.make_async_remote_copy(
                src_ref=parts.at[tp_me, t], dst_ref=parts.at[source, t], send_sem=part_send.at[k - 1, t],
                recv_sem=part_recv.at[source, t], device_id={"tp": source}, device_id_type=MESH,
            ).wait_recv()
        total = parts[0, t].astype(jnp.float32)
        for k in range(1, tp_n):
            total = total + parts[k, t].astype(jnp.float32)
        for p in range(problems):
            mixed = hidden[p, :, at].astype(jnp.float32) + total[p * steps:(p + 1) * steps]
            out[p, :, at] = mixed.astype(jnp.bfloat16)
        return carry

    lax.fori_loop(0, tiles, gather, 0)

    def rest(j):
        sibling_copy(j).wait_send()
        drain0(j)
        drain1(j)
        fork_copy(j).wait_send()

    loop(rest, chunks)

    def rest_parts(t, carry):
        for k in range(1, tp_n):
            part_copy(t, k).wait_send()
        return carry

    lax.fori_loop(0, tiles, rest_parts, 0)


def local(cand_n, tp_n, hidden_in, queries, new_kv, kv_cache, lengths, winner, out_values, out_scales):
    problems, kv_here, _, slots, head_dim = kv_cache.shape
    steps, heads = queries.shape[1:3]
    depth, width = out_values.shape
    rows = problems * steps
    split = 2 if kv_here % 2 == 0 else 1
    chunks = problems // 2 * split
    tile = 512
    tiles = width // tile
    flat = queries.reshape(problems, steps * heads, head_dim)
    fresh = jnp.transpose(new_kv, (0, 3, 2, 1, 4))
    fresh = fresh.reshape(problems, 2, kv_here * steps, head_dim)
    smem = pl.BlockSpec(memory_space=pltpu.SMEM)
    vmem = pl.BlockSpec(memory_space=pltpu.VMEM)
    hbm = pl.BlockSpec(memory_space=pl.ANY)
    line = pltpu.VMEM((chunks, kv_here // split, 2, BLOCK, head_dim), jnp.bfloat16)
    stat = pltpu.VMEM((problems, steps * heads, head_dim), jnp.float32)
    dma = pltpu.SemaphoreType.DMA
    blocks = pl.pallas_call(
        pick_kernel,
        out_shape=jax.ShapeDtypeStruct((problems * split, kv_here // split, 2, BLOCK, head_dim), jnp.bfloat16),
        in_specs=[smem, smem, hbm],
        out_specs=vmem,
        scratch_shapes=[
            pltpu.VMEM((problems, kv_here, 2, WINDOW, head_dim), jnp.bfloat16), dma((problems,)),
        ],
        compiler_params=pltpu.CompilerParams(vmem_limit_bytes=16 << 20),
    )(lengths, winner, kv_cache)
    return pl.pallas_call(
        functools.partial(kernel, cand_n, tp_n, tile, split),
        out_shape=jax.ShapeDtypeStruct(hidden_in.shape, jnp.bfloat16),
        in_specs=[smem, smem, vmem, vmem, vmem, vmem, hbm, hbm],
        out_specs=vmem,
        scratch_shapes=[
            pltpu.VMEM(kv_cache.shape, jnp.bfloat16),
            pltpu.VMEM(out_values.shape, jnp.bfloat16),
            *[line] * 11,
            pltpu.VMEM((problems * split, kv_here // split, 2, BLOCK, head_dim), jnp.bfloat16),
            stat, stat, stat,
            pltpu.VMEM((problems * steps * heads, head_dim), jnp.float32),
            pltpu.VMEM((heads // 2, 2 * rows, 2 * head_dim), jnp.bfloat16),
            pltpu.VMEM((tp_n, tiles, rows, tile), jnp.bfloat16),
            dma((problems,)), dma((8,)), dma((8, chunks)), dma((8, chunks)),
            dma((max(tp_n - 1, 1), tiles)), dma((tp_n, tiles)),
        ],
        compiler_params=pltpu.CompilerParams(
            collective_id=0, has_side_effects=True, vmem_limit_bytes=67043328 - (2 << 20)
        ),
    )(lengths, out_scales, blocks, flat, fresh, hidden_in, kv_cache, out_values)


def solution(mesh):
    placed = (
        P("cand", None, None),
        P("cand", None, "tp", None),
        P("cand", None, "tp", None, None),
        P("cand", "tp", None, None, None),
        P("cand"),
        P(),
        P("tp", None),
        P("tp", None),
    )
    return jax.shard_map(
        functools.partial(local, mesh.shape["cand"], mesh.shape["tp"]),
        mesh=mesh, in_specs=placed, out_specs=P("cand", None, None), check_vma=False,
    )
```

```python
import functools
import math

import jax
import jax.numpy as jnp
from jax import lax
from jax.experimental import pallas as pl
from jax.experimental.pallas import tpu as pltpu
from jax.sharding import PartitionSpec as P

BLOCK = 64
WINDOW = 128
LAG = 2
PAD = 16
LOW = -1e30
MESH = pl.DeviceIdType.MESH


def pick_kernel(lengths, winner, cache_hbm, blocks, held, sem):
    problems, kv_here, _, window, _ = held.shape
    slots = cache_hbm.shape[3]
    hs = blocks.shape[1]
    split = kv_here // hs
    me = lax.axis_index("cand")

    def begin_of(p):
        begin = lengths[p] - BLOCK
        base = jnp.clip(lax.div(begin, PAD) * PAD, 0, slots - window)
        return begin, pl.multiple_of(base, PAD)

    def fetch(p):
        base = begin_of(p)[1]
        return pltpu.make_async_copy(
            cache_hbm.at[p, :, :, pl.ds(base, window), :], held.at[p], sem.at[p]
        )

    for p in range(problems):
        fetch(p).start()
    row = lax.broadcasted_iota(jnp.int32, (BLOCK, window), 0)
    col = lax.broadcasted_iota(jnp.int32, (BLOCK, window), 1)
    for p in range(problems):
        fetch(p).wait()
        begin, base = begin_of(p)
        shift = jnp.where(winner[p] == me, begin - base, 4 * window)
        pick = (col == row + shift).astype(jnp.float32).astype(jnp.bfloat16)
        for h in range(kv_here):
            for kv in range(2):
                blocks[p * split + h // hs, h % hs, kv] = jnp.dot(
                    pick, held[p, h, kv], preferred_element_type=jnp.float32
                ).astype(jnp.bfloat16)


def kernel(
    cand_n, tp_n, tile, split,
    lengths, scales, blocks, queries, fresh, hidden, cache_hbm, weights_hbm, out,
    cache, weights, got, own, near0, up0, far0, down0, mid, near1, up1, far1, down1,
    fork, top_s, sum_s, acc_s, att, lhs, parts,
    cache_sem, weight_sem, send_sem, recv_sem, part_send, part_recv,
):
    me = lax.axis_index("cand")
    tp_me = lax.axis_index("tp")
    problems, kv_here, _, slots, head_dim = cache.shape
    steps_heads = queries.shape[1]
    heads = weights.shape[0] // head_dim
    steps = steps_heads // heads
    group = heads // kv_here
    rows = problems * steps
    half = problems // 2
    hs = kv_here // split
    chunks = half * split
    core = lax.rem(me, 2)
    chip = lax.div(me, 2)
    outer_len = 4
    inner_len = cand_n // 2 // outer_len
    inner_at = lax.rem(chip, inner_len)
    outer_at = lax.div(chip, inner_len)
    sibling = me + 1 - 2 * core

    def ends(at, length, stride):
        low_side = at < length // 2
        step = jnp.where(low_side, stride, -stride)
        has_near = jnp.logical_and(at > 0, at < length - 1)
        crosses = jnp.logical_or(at == length // 2 - 1, at == length // 2)
        return has_near, crosses, me + step, me - step

    inner = ends(inner_at, inner_len, 2)
    outer = ends(outer_at, outer_len, 2 * inner_len)

    barrier = pltpu.get_barrier_semaphore()

    def greet(**where):
        pl.semaphore_signal(barrier, inc=1, device_id=where, device_id_type=MESH)

    greet(cand=sibling)
    count = 1 + (tp_n - 1)
    for has_near, _, far, near in (inner, outer):
        greet(cand=far)

        @pl.when(has_near)
        def _(near=near):
            greet(cand=near)

        count = count + 1 + has_near.astype(jnp.int32)
    for k in range(1, tp_n):
        greet(tp=lax.rem(tp_me + k, tp_n))

    pieces = weight_sem.shape[0]
    piece = weights.shape[0] // pieces

    def cache_copy(p):
        return pltpu.make_async_copy(cache_hbm.at[p], cache.at[p], cache_sem.at[p])

    def weight_copy(i):
        at = pl.ds(i * piece, piece)
        return pltpu.make_async_copy(weights_hbm.at[at], weights.at[at], weight_sem.at[i])

    for p in range(problems):
        cache_copy(p).start()
    pl.semaphore_wait(barrier, count)

    def remote(src, dst, kind, j, target):
        return pltpu.make_async_remote_copy(
            src_ref=src, dst_ref=dst, send_sem=send_sem.at[kind, j],
            recv_sem=recv_sem.at[kind, j], device_id={"cand": target}, device_id_type=MESH,
        )

    def sibling_copy(j):
        return remote(blocks.at[(1 - core) * chunks + j], got.at[j], 0, j, sibling)

    def loop(body, length):
        def step(j, carry):
            body(j)
            return carry

        lax.fori_loop(0, length, step, 0)

    loop(lambda j: sibling_copy(j).start(), chunks)

    def make_line(line, kind, base_ref, near_ref, up_ref, far_ref, down_ref):
        has_near, crosses, far_id, near_id = line

        def to_far_in(j):
            return remote(up_ref.at[j], near_ref.at[j], kind, j, far_id)

        def to_far_cross(j):
            return remote(up_ref.at[j], far_ref.at[j], kind + 1, j, far_id)

        def to_near(j):
            return remote(down_ref.at[j], far_ref.at[j], kind + 1, j, near_id)

        def climb(j):
            @pl.when(has_near)
            def _():
                to_far_in(j).wait_recv()
                up_ref[j] = base_ref[j] + near_ref[j]

            @pl.when(jnp.logical_not(has_near))
            def _():
                up_ref[j] = base_ref[j]

            @pl.when(crosses)
            def _():
                to_far_cross(j).start()

            @pl.when(jnp.logical_not(crosses))
            def _():
                to_far_in(j).start()

        def settle(j):
            to_far_cross(j).wait_recv()

            @pl.when(has_near)
            def _():
                down_ref[j] = base_ref[j] + far_ref[j]
                pltpu.make_async_remote_copy(
                    src_ref=down_ref.at[j], dst_ref=far_ref.at[j], send_sem=send_sem.at[kind + 2, j],
                    recv_sem=recv_sem.at[kind + 1, j], device_id={"cand": near_id}, device_id_type=MESH,
                ).start()

            return up_ref[j] + far_ref[j]

        def drain(j):
            @pl.when(crosses)
            def _():
                to_far_cross(j).wait_send()

            @pl.when(jnp.logical_not(crosses))
            def _():
                to_far_in(j).wait_send()

            @pl.when(has_near)
            def _():
                remote(down_ref.at[j], far_ref.at[j], kind + 2, j, near_id).wait_send()

        return climb, settle, drain

    climb0, settle0, drain0 = make_line(inner, 1, own, near0, up0, far0, down0)
    climb1, settle1, drain1 = make_line(outer, 4, mid, near1, up1, far1, down1)

    def enter(j):
        sibling_copy(j).wait_recv()
        own[j] = blocks[core * chunks + j] + got[j]
        climb0(j)

    loop(enter, chunks)
    for i in range(pieces):
        weight_copy(i).start()

    factor = 1.0 / math.sqrt(head_dim)

    def row_of(width):
        return lax.broadcasted_iota(jnp.int32, (steps_heads, width), 0)

    def col_of(width):
        return lax.broadcasted_iota(jnp.int32, (steps_heads, width), 1)

    def score(q, keys):
        return lax.dot_general(q, keys, (((1,), (1,)), ((), ())), preferred_element_type=jnp.float32) * factor

    def local_part(p):
        cache_copy(p).wait()
        q = queries[p]
        s = score(q, cache[p, :, 0].reshape(kv_here * slots, head_dim))
        row, col = row_of(kv_here * slots), col_of(kv_here * slots)
        mine = lax.div(lax.rem(row, heads), group) == lax.div(col, slots)
        s = jnp.where(jnp.logical_and(mine, lax.rem(col, slots) < lengths[p] - BLOCK), s, LOW)
        n = score(q, fresh[p, 0])
        width = fresh.shape[2]
        row, col = row_of(width), col_of(width)
        mine = lax.div(lax.rem(row, heads), group) == lax.div(col, steps)
        n = jnp.where(jnp.logical_and(mine, lax.rem(col, steps) <= lax.div(row, heads)), n, LOW)
        top = jnp.maximum(jnp.max(s, 1, keepdims=True), jnp.max(n, 1, keepdims=True))
        s = jnp.exp(s - top)
        n = jnp.exp(n - top)
        top_s[p] = jnp.broadcast_to(top, (steps_heads, head_dim))
        sum_s[p] = jnp.broadcast_to(jnp.sum(s, 1, keepdims=True) + jnp.sum(n, 1, keepdims=True), (steps_heads, head_dim))
        acc_s[p] = jnp.dot(
            s.astype(jnp.bfloat16), cache[p, :, 1].reshape(kv_here * slots, head_dim),
            preferred_element_type=jnp.float32,
        ) + jnp.dot(n.astype(jnp.bfloat16), fresh[p, 1], preferred_element_type=jnp.float32)

    def turn(j):
        mid[j] = settle0(j)
        climb1(j)


    def fork_copy(j):
        at = core * chunks + j
        return remote(fork.at[at], fork.at[at], 7, j, sibling)

    def finish(j):
        fork[core * chunks + j] = settle1(j)
        fork_copy(j).start()

    each = pl.cdiv(problems, chunks)

    def advance(j):
        @pl.when(j < chunks)
        def _():
            turn(j)

        for i in range(each):
            @pl.when(j * each + i < problems)
            def _(i=i):
                local_part(j * each + i)

        @pl.when(jnp.logical_and(j >= lag, j < chunks + lag))
        def _():
            finish(j - lag)

    lag = jnp.where(outer[0], LAG, chunks)
    loop(advance, 2 * chunks)

    def closing(j):
        remote(got.at[j], fork.at[(1 - core) * chunks + j], 7, j, sibling).wait_recv()

    loop(closing, chunks)

    def fork_part(p, carry):
        q = queries[p]
        both = fork[pl.ds(p * split, split)]
        keys = both[:, :, 0].reshape(kv_here * BLOCK, head_dim)
        values = both[:, :, 1].reshape(kv_here * BLOCK, head_dim)
        s = score(q, keys)
        row, col = row_of(kv_here * BLOCK), col_of(kv_here * BLOCK)
        mine = lax.div(lax.rem(row, heads), group) == lax.div(col, BLOCK)
        s = jnp.where(mine, s, LOW)
        before = top_s[p]
        top = jnp.maximum(before, jnp.max(s, 1, keepdims=True))
        s = jnp.exp(s - top[:, :1])
        scale = jnp.exp(before - top)
        total = sum_s[p] * scale + jnp.sum(s, 1, keepdims=True)
        acc = acc_s[p] * scale + jnp.dot(s.astype(jnp.bfloat16), values, preferred_element_type=jnp.float32)
        att[pl.ds(p * steps_heads, steps_heads), :] = acc / total
        return carry

    lax.fori_loop(0, problems, fork_part, 0)

    pairs = heads // 2
    empty = jnp.zeros((rows, head_dim), jnp.bfloat16)
    for i in range(pairs):
        a = att[pl.ds(2 * i, rows, stride=heads), :].astype(jnp.bfloat16)
        b = att[pl.ds(2 * i + 1, rows, stride=heads), :].astype(jnp.bfloat16)
        lhs[i] = jnp.concatenate(
            [jnp.concatenate([a, empty], 1), jnp.concatenate([empty, b], 1)], 0
        )

    for i in range(pieces):
        weight_copy(i).wait()

    tiles = parts.shape[1]
    per = tile // head_dim

    def part_copy(t, k):
        return pltpu.make_async_remote_copy(
            src_ref=parts.at[tp_me, t], dst_ref=parts.at[tp_me, t], send_sem=part_send.at[k - 1, t],
            recv_sem=part_recv.at[tp_me, t], device_id={"tp": lax.rem(tp_me + k, tp_n)},
            device_id_type=MESH,
        )

    def project(t, carry):
        at = pl.ds(pl.multiple_of(t * tile, tile), tile)
        total = [jnp.zeros((rows, head_dim), jnp.float32) for _ in range(per)]
        for i in range(pairs):
            product = jnp.dot(
                lhs[i], weights[pl.ds(2 * i * head_dim, 2 * head_dim), at], preferred_element_type=jnp.float32
            )
            for c in range(per):
                here = product[:, c * head_dim:(c + 1) * head_dim]
                total[c] = (
                    total[c] + here[:rows] * scales[2 * i, t * per + c]
                    + here[rows:] * scales[2 * i + 1, t * per + c]
                )
        parts[tp_me, t] = jnp.concatenate(total, 1).astype(jnp.bfloat16)
        for k in range(1, tp_n):
            part_copy(t, k).start()
        return carry

    lax.fori_loop(0, tiles, project, 0)

    def gather(t, carry):
        at = pl.ds(pl.multiple_of(t * tile, tile), tile)
        for k in range(1, tp_n):
            source = lax.rem(tp_me + k, tp_n)
            pltpu.make_async_remote_copy(
                src_ref=parts.at[tp_me, t], dst_ref=parts.at[source, t], send_sem=part_send.at[k - 1, t],
                recv_sem=part_recv.at[source, t], device_id={"tp": source}, device_id_type=MESH,
            ).wait_recv()
        total = parts[0, t].astype(jnp.float32)
        for k in range(1, tp_n):
            total = total + parts[k, t].astype(jnp.float32)
        for p in range(problems):
            mixed = hidden[p, :, at].astype(jnp.float32) + total[p * steps:(p + 1) * steps]
            out[p, :, at] = mixed.astype(jnp.bfloat16)
        return carry

    lax.fori_loop(0, tiles, gather, 0)

    def rest(j):
        sibling_copy(j).wait_send()
        drain0(j)
        drain1(j)
        fork_copy(j).wait_send()

    loop(rest, chunks)

    def rest_parts(t, carry):
        for k in range(1, tp_n):
            part_copy(t, k).wait_send()
        return carry

    lax.fori_loop(0, tiles, rest_parts, 0)


def local(cand_n, tp_n, hidden_in, queries, new_kv, kv_cache, lengths, winner, out_values, out_scales):
    problems, kv_here, _, slots, head_dim = kv_cache.shape
    steps, heads = queries.shape[1:3]
    depth, width = out_values.shape
    rows = problems * steps
    split = 2 if kv_here % 2 == 0 else 1
    chunks = problems // 2 * split
    tile = 512
    tiles = width // tile
    flat = queries.reshape(problems, steps * heads, head_dim)
    fresh = jnp.transpose(new_kv, (0, 3, 2, 1, 4))
    fresh = fresh.reshape(problems, 2, kv_here * steps, head_dim)
    smem = pl.BlockSpec(memory_space=pltpu.SMEM)
    vmem = pl.BlockSpec(memory_space=pltpu.VMEM)
    hbm = pl.BlockSpec(memory_space=pl.ANY)
    line = pltpu.VMEM((chunks, kv_here // split, 2, BLOCK, head_dim), jnp.bfloat16)
    stat = pltpu.VMEM((problems, steps * heads, head_dim), jnp.float32)
    dma = pltpu.SemaphoreType.DMA
    blocks = pl.pallas_call(
        pick_kernel,
        out_shape=jax.ShapeDtypeStruct((problems * split, kv_here // split, 2, BLOCK, head_dim), jnp.bfloat16),
        in_specs=[smem, smem, hbm],
        out_specs=vmem,
        scratch_shapes=[
            pltpu.VMEM((problems, kv_here, 2, WINDOW, head_dim), jnp.bfloat16), dma((problems,)),
        ],
        compiler_params=pltpu.CompilerParams(vmem_limit_bytes=67043328 - (2 << 20)),
    )(lengths, winner, kv_cache)
    return pl.pallas_call(
        functools.partial(kernel, cand_n, tp_n, tile, split),
        out_shape=jax.ShapeDtypeStruct(hidden_in.shape, jnp.bfloat16),
        in_specs=[smem, smem, vmem, vmem, vmem, vmem, hbm, hbm],
        out_specs=vmem,
        scratch_shapes=[
            pltpu.VMEM(kv_cache.shape, jnp.bfloat16),
            pltpu.VMEM(out_values.shape, jnp.bfloat16),
            *[line] * 11,
            pltpu.VMEM((problems * split, kv_here // split, 2, BLOCK, head_dim), jnp.bfloat16),
            stat, stat, stat,
            pltpu.VMEM((problems * steps * heads, head_dim), jnp.float32),
            pltpu.VMEM((heads // 2, 2 * rows, 2 * head_dim), jnp.bfloat16),
            pltpu.VMEM((tp_n, tiles, rows, tile), jnp.bfloat16),
            dma((problems,)), dma((8,)), dma((8, chunks)), dma((8, chunks)),
            dma((max(tp_n - 1, 1), tiles)), dma((tp_n, tiles)),
        ],
        compiler_params=pltpu.CompilerParams(
            collective_id=0, has_side_effects=True, vmem_limit_bytes=67043328 - (2 << 20)
        ),
    )(lengths, out_scales, blocks, flat, fresh, hidden_in, kv_cache, out_values)


def solution(mesh):
    placed = (
        P("cand", None, None),
        P("cand", None, "tp", None),
        P("cand", None, "tp", None, None),
        P("cand", "tp", None, None, None),
        P("cand"),
        P(),
        P("tp", None),
        P("tp", None),
    )
    return jax.shard_map(
        functools.partial(local, mesh.shape["cand"], mesh.shape["tp"]),
        mesh=mesh, in_specs=placed, out_specs=P("cand", None, None), check_vma=False,
    )
```

```python
import functools
import math

import jax
import jax.numpy as jnp
from jax import lax
from jax.experimental import pallas as pl
from jax.experimental.pallas import tpu as pltpu
from jax.sharding import PartitionSpec as P

BLOCK = 64
WINDOW = 128
LAG = 2
PAD = 16
LOW = -1e30
MESH = pl.DeviceIdType.MESH


def pick_kernel(lengths, winner, cache_hbm, blocks, held, sem):
    problems, kv_here, _, window, _ = held.shape
    slots = cache_hbm.shape[3]
    hs = blocks.shape[1]
    split = kv_here // hs
    me = lax.axis_index("cand")

    def begin_of(p):
        begin = lengths[p] - BLOCK
        base = jnp.clip(lax.div(begin, PAD) * PAD, 0, slots - window)
        return begin, pl.multiple_of(base, PAD)

    def fetch(p):
        base = begin_of(p)[1]
        return pltpu.make_async_copy(
            cache_hbm.at[p, :, :, pl.ds(base, window), :], held.at[p], sem.at[p]
        )

    for p in range(problems):
        fetch(p).start()
    row = lax.broadcasted_iota(jnp.int32, (BLOCK, window), 0)
    col = lax.broadcasted_iota(jnp.int32, (BLOCK, window), 1)
    for p in range(problems):
        fetch(p).wait()
        begin, base = begin_of(p)
        shift = jnp.where(winner[p] == me, begin - base, 4 * window)
        pick = (col == row + shift).astype(jnp.float32).astype(jnp.bfloat16)
        for h in range(kv_here):
            for kv in range(2):
                blocks[p * split + h // hs, h % hs, kv] = jnp.dot(
                    pick, held[p, h, kv], preferred_element_type=jnp.float32
                ).astype(jnp.bfloat16)


def kernel(
    cand_n, tp_n, tile, split,
    lengths, scales, blocks, queries, fresh, hidden, cache_hbm, weights_hbm, out,
    cache, weights, got, own, near0, up0, far0, down0, mid, near1, up1, far1, down1,
    fork, top_s, sum_s, acc_s, att, lhs, parts, other,
    cache_sem, weight_sem, send_sem, recv_sem, part_send, part_recv, swap_sem, other_send,
):
    me = lax.axis_index("cand")
    tp_me = lax.axis_index("tp")
    problems, kv_here, _, slots, head_dim = cache.shape
    steps_heads = queries.shape[1]
    heads = weights.shape[0] // head_dim
    steps = steps_heads // heads
    group = heads // kv_here
    rows = problems * steps
    half = problems // 2
    hs = kv_here // split
    chunks = half * split
    core = lax.rem(me, 2)
    chip = lax.div(me, 2)
    outer_len = 4
    inner_len = cand_n // 2 // outer_len
    inner_at = lax.rem(chip, inner_len)
    outer_at = lax.div(chip, inner_len)
    sibling = me + 1 - 2 * core

    def ends(at, length, stride):
        low_side = at < length // 2
        step = jnp.where(low_side, stride, -stride)
        has_near = jnp.logical_and(at > 0, at < length - 1)
        crosses = jnp.logical_or(at == length // 2 - 1, at == length // 2)
        return has_near, crosses, me + step, me - step

    inner = ends(inner_at, inner_len, 2)
    outer = ends(outer_at, outer_len, 2 * inner_len)

    barrier = pltpu.get_barrier_semaphore()

    def greet(**where):
        pl.semaphore_signal(barrier, inc=1, device_id=where, device_id_type=MESH)

    greet(cand=sibling)
    count = 1 + 2 * (tp_n - 1)
    for has_near, _, far, near in (inner, outer):
        greet(cand=far)

        @pl.when(has_near)
        def _(near=near):
            greet(cand=near)

        count = count + 1 + has_near.astype(jnp.int32)
    for k in range(1, tp_n):
        greet(tp=lax.rem(tp_me + k, tp_n))
        greet(cand=sibling, tp=lax.rem(tp_me + k, tp_n))

    pieces = weight_sem.shape[0]
    piece = weights.shape[0] // pieces

    def cache_copy(p):
        return pltpu.make_async_copy(cache_hbm.at[p], cache.at[p], cache_sem.at[p])

    def weight_copy(i):
        at = pl.ds(i * piece, piece)
        columns = pl.ds(pl.multiple_of(core * weights.shape[1], tile), weights.shape[1])
        return pltpu.make_async_copy(weights_hbm.at[at, columns], weights.at[at], weight_sem.at[i])

    for p in range(problems):
        cache_copy(p).start()
    pl.semaphore_wait(barrier, count)

    def remote(src, dst, kind, j, target):
        return pltpu.make_async_remote_copy(
            src_ref=src, dst_ref=dst, send_sem=send_sem.at[kind, j],
            recv_sem=recv_sem.at[kind, j], device_id={"cand": target}, device_id_type=MESH,
        )

    def sibling_copy(j):
        return remote(blocks.at[(1 - core) * chunks + j], got.at[j], 0, j, sibling)

    def loop(body, length):
        def step(j, carry):
            body(j)
            return carry

        lax.fori_loop(0, length, step, 0)

    loop(lambda j: sibling_copy(j).start(), chunks)

    def make_line(line, kind, base_ref, near_ref, up_ref, far_ref, down_ref):
        has_near, crosses, far_id, near_id = line

        def to_far_in(j):
            return remote(up_ref.at[j], near_ref.at[j], kind, j, far_id)

        def to_far_cross(j):
            return remote(up_ref.at[j], far_ref.at[j], kind + 1, j, far_id)

        def to_near(j):
            return remote(down_ref.at[j], far_ref.at[j], kind + 1, j, near_id)

        def climb(j):
            @pl.when(has_near)
            def _():
                to_far_in(j).wait_recv()
                up_ref[j] = base_ref[j] + near_ref[j]

            @pl.when(jnp.logical_not(has_near))
            def _():
                up_ref[j] = base_ref[j]

            @pl.when(crosses)
            def _():
                to_far_cross(j).start()

            @pl.when(jnp.logical_not(crosses))
            def _():
                to_far_in(j).start()

        def settle(j):
            to_far_cross(j).wait_recv()

            @pl.when(has_near)
            def _():
                down_ref[j] = base_ref[j] + far_ref[j]
                pltpu.make_async_remote_copy(
                    src_ref=down_ref.at[j], dst_ref=far_ref.at[j], send_sem=send_sem.at[kind + 2, j],
                    recv_sem=recv_sem.at[kind + 1, j], device_id={"cand": near_id}, device_id_type=MESH,
                ).start()

            return up_ref[j] + far_ref[j]

        def drain(j):
            @pl.when(crosses)
            def _():
                to_far_cross(j).wait_send()

            @pl.when(jnp.logical_not(crosses))
            def _():
                to_far_in(j).wait_send()

            @pl.when(has_near)
            def _():
                remote(down_ref.at[j], far_ref.at[j], kind + 2, j, near_id).wait_send()

        return climb, settle, drain

    climb0, settle0, drain0 = make_line(inner, 1, own, near0, up0, far0, down0)
    climb1, settle1, drain1 = make_line(outer, 4, mid, near1, up1, far1, down1)

    def enter(j):
        sibling_copy(j).wait_recv()
        own[j] = blocks[core * chunks + j] + got[j]
        climb0(j)

    loop(enter, chunks)
    for i in range(pieces):
        weight_copy(i).start()

    factor = 1.0 / math.sqrt(head_dim)

    def row_of(width):
        return lax.broadcasted_iota(jnp.int32, (steps_heads, width), 0)

    def col_of(width):
        return lax.broadcasted_iota(jnp.int32, (steps_heads, width), 1)

    def score(q, keys):
        return lax.dot_general(q, keys, (((1,), (1,)), ((), ())), preferred_element_type=jnp.float32) * factor

    def local_part(p):
        cache_copy(p).wait()
        q = queries[p]
        s = score(q, cache[p, :, 0].reshape(kv_here * slots, head_dim))
        row, col = row_of(kv_here * slots), col_of(kv_here * slots)
        mine = lax.div(lax.rem(row, heads), group) == lax.div(col, slots)
        s = jnp.where(jnp.logical_and(mine, lax.rem(col, slots) < lengths[p] - BLOCK), s, LOW)
        n = score(q, fresh[p, 0])
        width = fresh.shape[2]
        row, col = row_of(width), col_of(width)
        mine = lax.div(lax.rem(row, heads), group) == lax.div(col, steps)
        n = jnp.where(jnp.logical_and(mine, lax.rem(col, steps) <= lax.div(row, heads)), n, LOW)
        top = jnp.maximum(jnp.max(s, 1, keepdims=True), jnp.max(n, 1, keepdims=True))
        s = jnp.exp(s - top)
        n = jnp.exp(n - top)
        top_s[p] = jnp.broadcast_to(top, (steps_heads, head_dim))
        sum_s[p] = jnp.broadcast_to(jnp.sum(s, 1, keepdims=True) + jnp.sum(n, 1, keepdims=True), (steps_heads, head_dim))
        acc_s[p] = jnp.dot(
            s.astype(jnp.bfloat16), cache[p, :, 1].reshape(kv_here * slots, head_dim),
            preferred_element_type=jnp.float32,
        ) + jnp.dot(n.astype(jnp.bfloat16), fresh[p, 1], preferred_element_type=jnp.float32)

    def turn(j):
        mid[j] = settle0(j)
        climb1(j)


    def fork_copy(j):
        at = core * chunks + j
        return remote(fork.at[at], fork.at[at], 7, j, sibling)

    def finish(j):
        fork[core * chunks + j] = settle1(j)
        fork_copy(j).start()

    each = pl.cdiv(problems, chunks)

    def advance(j):
        @pl.when(j < chunks)
        def _():
            turn(j)

        for i in range(each):
            @pl.when(j * each + i < problems)
            def _(i=i):
                local_part(j * each + i)

        @pl.when(jnp.logical_and(j >= lag, j < chunks + lag))
        def _():
            finish(j - lag)

    lag = jnp.where(outer[0], LAG, chunks)
    loop(advance, 2 * chunks)

    def closing(j):
        remote(got.at[j], fork.at[(1 - core) * chunks + j], 7, j, sibling).wait_recv()

    loop(closing, chunks)

    def fork_part(p, carry):
        q = queries[p]
        both = fork[pl.ds(p * split, split)]
        keys = both[:, :, 0].reshape(kv_here * BLOCK, head_dim)
        values = both[:, :, 1].reshape(kv_here * BLOCK, head_dim)
        s = score(q, keys)
        row, col = row_of(kv_here * BLOCK), col_of(kv_here * BLOCK)
        mine = lax.div(lax.rem(row, heads), group) == lax.div(col, BLOCK)
        s = jnp.where(mine, s, LOW)
        before = top_s[p]
        top = jnp.maximum(before, jnp.max(s, 1, keepdims=True))
        s = jnp.exp(s - top[:, :1])
        scale = jnp.exp(before - top)
        total = sum_s[p] * scale + jnp.sum(s, 1, keepdims=True)
        acc = acc_s[p] * scale + jnp.dot(s.astype(jnp.bfloat16), values, preferred_element_type=jnp.float32)
        att[pl.ds(p * steps_heads, steps_heads), :] = acc / total
        return carry

    lax.fori_loop(0, problems, fork_part, 0)

    pairs = heads // 2
    empty = jnp.zeros((rows, head_dim), jnp.bfloat16)
    for i in range(pairs):
        a = att[pl.ds(2 * i, rows, stride=heads), :].astype(jnp.bfloat16)
        b = att[pl.ds(2 * i + 1, rows, stride=heads), :].astype(jnp.bfloat16)
        lhs[0, i] = jnp.concatenate(
            [jnp.concatenate([a, empty], 1), jnp.concatenate([empty, b], 1)], 0
        )

    swap = pltpu.make_async_remote_copy(
        src_ref=lhs.at[0], dst_ref=lhs.at[1], send_sem=swap_sem.at[0], recv_sem=swap_sem.at[1],
        device_id={"cand": sibling}, device_id_type=MESH,
    )
    swap.start()
    for i in range(pieces):
        weight_copy(i).wait()
    swap.wait_recv()

    tiles = parts.shape[1]
    here_tiles = tiles // 2
    per = tile // head_dim

    def part_copy(t, k):
        at = core * here_tiles + t
        return pltpu.make_async_remote_copy(
            src_ref=parts.at[tp_me, at], dst_ref=parts.at[tp_me, at], send_sem=part_send.at[k - 1, t],
            recv_sem=part_recv.at[tp_me, at], device_id={"tp": lax.rem(tp_me + k, tp_n)},
            device_id_type=MESH,
        )

    def other_copy(t, k):
        at = core * here_tiles + t
        return pltpu.make_async_remote_copy(
            src_ref=other.at[t], dst_ref=parts.at[tp_me, at], send_sem=other_send.at[k, t],
            recv_sem=part_recv.at[tp_me, at],
            device_id={"cand": sibling, "tp": lax.rem(tp_me + k, tp_n)}, device_id_type=MESH,
        )

    def project(t, carry):
        at = pl.ds(pl.multiple_of(t * tile, tile), tile)
        first_scale = (core * here_tiles + t) * per
        total = [jnp.zeros((2, rows, head_dim), jnp.float32) for _ in range(per)]
        for i in range(pairs):
            product = jnp.dot(
                lhs[:, i].reshape(4 * rows, 2 * head_dim),
                weights[pl.ds(2 * i * head_dim, 2 * head_dim), at], preferred_element_type=jnp.float32,
            )
            for c in range(per):
                here = product[:, c * head_dim:(c + 1) * head_dim].reshape(2, 2, rows, head_dim)
                total[c] = (
                    total[c] + here[:, 0] * scales[2 * i, first_scale + c]
                    + here[:, 1] * scales[2 * i + 1, first_scale + c]
                )
        whole = jnp.concatenate(total, 2).astype(jnp.bfloat16)
        parts[tp_me, core * here_tiles + t] = whole[0]
        other[t] = whole[1]
        for k in range(1, tp_n):
            other_copy(t, k).start()
            part_copy(t, k).start()
        other_copy(t, 0).start()
        return carry

    lax.fori_loop(0, here_tiles, project, 0)

    def gather(t, carry):
        at = pl.ds(pl.multiple_of(t * tile, tile), tile)

        def arrived(source):
            pltpu.make_async_remote_copy(
                src_ref=other.at[0], dst_ref=parts.at[source, t], send_sem=swap_sem.at[0],
                recv_sem=part_recv.at[source, t], device_id={"cand": sibling}, device_id_type=MESH,
            ).wait_recv()

        @pl.when(lax.div(t, here_tiles) != core)
        def _():
            arrived(tp_me)

        for k in range(1, tp_n):
            arrived(lax.rem(tp_me + k, tp_n))
        total = parts[0, t].astype(jnp.float32)
        for k in range(1, tp_n):
            total = total + parts[k, t].astype(jnp.float32)
        for p in range(problems):
            mixed = hidden[p, :, at].astype(jnp.float32) + total[p * steps:(p + 1) * steps]
            out[p, :, at] = mixed.astype(jnp.bfloat16)
        return carry

    lax.fori_loop(0, tiles, gather, 0)
    swap.wait_send()

    def rest(j):
        sibling_copy(j).wait_send()
        drain0(j)
        drain1(j)
        fork_copy(j).wait_send()

    loop(rest, chunks)

    def rest_parts(t, carry):
        other_copy(t, 0).wait_send()
        for k in range(1, tp_n):
            part_copy(t, k).wait_send()
            other_copy(t, k).wait_send()
        return carry

    lax.fori_loop(0, here_tiles, rest_parts, 0)


def local(cand_n, tp_n, hidden_in, queries, new_kv, kv_cache, lengths, winner, out_values, out_scales):
    problems, kv_here, _, slots, head_dim = kv_cache.shape
    steps, heads = queries.shape[1:3]
    depth, width = out_values.shape
    rows = problems * steps
    split = 2 if kv_here % 2 == 0 else 1
    chunks = problems // 2 * split
    tile = 512
    tiles = width // tile
    flat = queries.reshape(problems, steps * heads, head_dim)
    fresh = jnp.transpose(new_kv, (0, 3, 2, 1, 4))
    fresh = fresh.reshape(problems, 2, kv_here * steps, head_dim)
    smem = pl.BlockSpec(memory_space=pltpu.SMEM)
    vmem = pl.BlockSpec(memory_space=pltpu.VMEM)
    hbm = pl.BlockSpec(memory_space=pl.ANY)
    line = pltpu.VMEM((chunks, kv_here // split, 2, BLOCK, head_dim), jnp.bfloat16)
    stat = pltpu.VMEM((problems, steps * heads, head_dim), jnp.float32)
    dma = pltpu.SemaphoreType.DMA
    blocks = pl.pallas_call(
        pick_kernel,
        out_shape=jax.ShapeDtypeStruct((problems * split, kv_here // split, 2, BLOCK, head_dim), jnp.bfloat16),
        in_specs=[smem, smem, hbm],
        out_specs=vmem,
        scratch_shapes=[
            pltpu.VMEM((problems, kv_here, 2, WINDOW, head_dim), jnp.bfloat16), dma((problems,)),
        ],
        compiler_params=pltpu.CompilerParams(vmem_limit_bytes=67043328 - (2 << 20)),
    )(lengths, winner, kv_cache)
    return pl.pallas_call(
        functools.partial(kernel, cand_n, tp_n, tile, split),
        out_shape=jax.ShapeDtypeStruct(hidden_in.shape, jnp.bfloat16),
        in_specs=[smem, smem, vmem, vmem, vmem, vmem, hbm, hbm],
        out_specs=vmem,
        scratch_shapes=[
            pltpu.VMEM(kv_cache.shape, jnp.bfloat16),
            pltpu.VMEM((depth, width // 2), jnp.bfloat16),
            *[line] * 11,
            pltpu.VMEM((problems * split, kv_here // split, 2, BLOCK, head_dim), jnp.bfloat16),
            stat, stat, stat,
            pltpu.VMEM((problems * steps * heads, head_dim), jnp.float32),
            pltpu.VMEM((2, heads // 2, 2 * rows, 2 * head_dim), jnp.bfloat16),
            pltpu.VMEM((tp_n, tiles, rows, tile), jnp.bfloat16),
            pltpu.VMEM((tiles // 2, rows, tile), jnp.bfloat16),
            dma((problems,)), dma((8,)), dma((8, chunks)), dma((8, chunks)),
            dma((max(tp_n - 1, 1), tiles // 2)), dma((tp_n, tiles)),
            dma((2,)), dma((tp_n, tiles // 2)),
        ],
        compiler_params=pltpu.CompilerParams(
            collective_id=0, has_side_effects=True, vmem_limit_bytes=67043328 - (2 << 20)
        ),
    )(lengths, out_scales, blocks, flat, fresh, hidden_in, kv_cache, out_values)


def solution(mesh):
    placed = (
        P("cand", None, None),
        P("cand", None, "tp", None),
        P("cand", None, "tp", None, None),
        P("cand", "tp", None, None, None),
        P("cand"),
        P(),
        P("tp", None),
        P("tp", None),
    )
    return jax.shard_map(
        functools.partial(local, mesh.shape["cand"], mesh.shape["tp"]),
        mesh=mesh, in_specs=placed, out_specs=P("cand", None, None), check_vma=False,
    )
```
